256 devices in a mesh: depth: 8 (over y, core), tile: 32 (over x, z).
Axes of the slice: x: 4, y: 4, z: 8, core: 2. Of those that a mesh axis runs over, the one named last changes fastest.
Arguments:
- density: int32 [256, 2048, 1024], P('depth', 'tile'), may hold values from 0 to 255
- view_flip: int32 [32], P('tile'), may hold values from 0 to 1
- tf_coeff: float32 [4, 4], replicated, may hold values from -4 to 4
Outputs:
- shaded: float32 [3, 2048, 1024], P(None, 'tile', 'depth')
The draws below stay inside these ranges and needn't reach their ends.
All inputs are finite; a program needn't handle non-finite values.
Results may differ from the reference program's by a relative error of at most 0.0003.
Values may be sent and summed in bfloat16 or wider, within the bound.
A program may use at most 192 MiB of HBM per device.

```python
import jax
import jax.numpy as jnp
from jax import lax

ROWS_DEV = 64
W = 1024
RADIUS = 8
DEG = 4
H = 2048
NZ = 256
N_TILE = 32


def octave(seed_key, period, amplitude):
    extents = ((NZ + period - 1) // period + 2, (H + period - 1) // period + 2, (W + period - 1) // period + 2)
    result = jax.random.randint(seed_key, extents, -amplitude, amplitude + 1, dtype=jnp.int32)
    for along_axis, length in ((0, NZ), (1, H), (2, W)):
        cell_index = jnp.arange(length, dtype=jnp.int32)
        lower_cell = cell_index // period
        fraction = cell_index % period
        view_shape = [1, 1, 1]
        view_shape[along_axis] = length
        fraction = fraction.reshape(view_shape)
        first = jnp.take(result, lower_cell, axis=along_axis)
        second = jnp.take(result, lower_cell + 1, axis=along_axis)
        result = (first * (period - fraction) + second * fraction) // period
    return result


def sphere_distance(seed_key, z_low, z_high):
    centre_z = jax.random.randint(jax.random.fold_in(seed_key, 1), (), z_low, z_high, dtype=jnp.int32)
    centre_y = jax.random.randint(jax.random.fold_in(seed_key, 2), (), 0, H, dtype=jnp.int32)
    centre_x = jax.random.randint(jax.random.fold_in(seed_key, 3), (), 0, W, dtype=jnp.int32)
    offset_z = jnp.arange(NZ, dtype=jnp.int32) - centre_z
    offset_y = jnp.arange(H, dtype=jnp.int32) - centre_y
    offset_x = jnp.arange(W, dtype=jnp.int32) - centre_x
    return (offset_z * offset_z)[:, None, None] + (offset_y * offset_y)[None, :, None] + (offset_x * offset_x)[None, None, :]


def draw_density(key, part):
    field = jnp.int32(110) + octave(jax.random.fold_in(key, 11), 64, 90)
    field = field + octave(jax.random.fold_in(key, 12), 16, 50)
    field = field + octave(jax.random.fold_in(key, 13), 4, 25)
    field = field + jax.random.randint(jax.random.fold_in(key, 14), (NZ, H, W), -12, 13, dtype=jnp.int32)
    for blob_number in range(6):
        blob_key = jax.random.fold_in(key, 100 + blob_number)
        distance = sphere_distance(blob_key, 0, NZ)
        radius = jax.random.randint(jax.random.fold_in(blob_key, 4), (), 6, 41, dtype=jnp.int32)
        polarity = 2 * jax.random.randint(jax.random.fold_in(blob_key, 5), (), 0, 2, dtype=jnp.int32) - 1
        hollow = jax.random.randint(jax.random.fold_in(blob_key, 6), (), 0, 2, dtype=jnp.int32)
        outer = (radius + 3) * (radius + 3)
        inner = jnp.where(hollow == 1, radius * radius, jnp.int32(0))
        inside = (distance <= outer) & (distance >= inner)
        field = field + jnp.where(inside, 70 * polarity, jnp.int32(0))
    dense_key = jax.random.fold_in(key, 200)
    dense_distance = sphere_distance(dense_key, 0, NZ // 4)
    dense_radius = jax.random.randint(jax.random.fold_in(dense_key, 4), (), 6, 17, dtype=jnp.int32)
    field = jnp.where(dense_distance <= dense_radius * dense_radius, jnp.int32(255), field)
    void_key = jax.random.fold_in(key, 201)
    void_distance = sphere_distance(void_key, 3 * NZ // 4, NZ)
    void_radius = jax.random.randint(jax.random.fold_in(void_key, 4), (), 6, 17, dtype=jnp.int32)
    field = jnp.where(void_distance <= void_radius * void_radius, jnp.int32(0), field)
    return jnp.clip(field, 0, 255).astype(jnp.int32)


def touch_ends(drawn, key, least, high):
    dims = drawn.shape
    spot = [jax.random.randint(jax.random.fold_in(key, axis), (), 0, dims[axis]) for axis in range(len(dims))]
    drawn = drawn.at[tuple(spot)].set(least)
    longest = dims.index(max(dims))
    spot[longest] = (spot[longest] + 1) % dims[longest]
    return drawn.at[tuple(spot)].set(high)


def normal_values(own_key, shape, scale, reach, kind=jnp.bfloat16):
    return jnp.clip(scale * jax.random.normal(own_key, shape, jnp.float32), -reach, reach).astype(kind)


def setup_inputs(seed: int = 0) -> dict:
    keys = jax.random.split(jax.random.key(seed), 4)
    density = draw_density(jax.random.fold_in(keys[3], 71), 0)
    view_flip = touch_ends(jax.random.randint(keys[1], (N_TILE,), 0, 2), jax.random.fold_in(keys[1], 1), 0, 1).astype(jnp.int32)
    tf_coeff = normal_values(keys[2], (4, DEG), 1.0, 4.0, jnp.float32)
    return {"density": density, "view_flip": view_flip, "tf_coeff": tf_coeff}


opacity_scale = 0.008
grad_half = 1.0
light_x = 0.48
light_y = 0.6
light_z = 0.64
spatial_scale = 1.0 / 72.0
depth_weight = 20.0
normal_weight = 2.0

def polynomial(coeff, scaled):
    return coeff[0] + scaled * (coeff[1] + scaled * (coeff[2] + scaled * coeff[3]))

def integrate(field, flipped, tf_coeff, depth_start, depth_total):
    centre = field[1:-1, 1:-1, :]
    sideways = jnp.pad(centre, ((0, 0), (0, 0), (1, 1)))
    grad_x = (sideways[:, :, 2:] - sideways[:, :, :-2]) * grad_half
    grad_y = (field[1:-1, 2:, :] - field[1:-1, :-2, :]) * grad_half
    grad_z = (field[2:, 1:-1, :] - field[:-2, 1:-1, :]) * grad_half
    scaling = lax.rsqrt(1.0 + grad_x * grad_x + grad_y * grad_y + grad_z * grad_z)
    normal_x = grad_x * scaling
    normal_y = grad_y * scaling
    normal_z = grad_z * scaling
    shading = 0.35 + 0.65 * jnp.abs(light_x * normal_x + light_y * normal_y + light_z * normal_z)
    scaled = 2.0 * centre - 1.0
    sigma = opacity_scale * jax.nn.softplus(polynomial(tf_coeff[0], scaled))
    running = jnp.cumsum(sigma, axis=0)
    total = running[-1]
    optical = jnp.where(flipped == 1, total - running, running - sigma)
    weight = jnp.exp(-optical) * (1.0 - jnp.exp(-sigma))
    cells = sigma.shape[0]
    height = ((depth_start + jnp.arange(cells, dtype=jnp.int32)).astype(jnp.float32) + 0.5) / depth_total
    height = jnp.where(flipped == 1, 1.0 - height, height)[:, None, None]
    planes = []
    for channel in range(1, 4):
        colour = jax.nn.sigmoid(polynomial(tf_coeff[channel], scaled)) * shading
        planes.append(lax.optimization_barrier(jnp.sum(weight * colour, axis=0)))
    planes.append(1.0 - jnp.exp(-total))
    planes.append(lax.optimization_barrier(jnp.sum(weight * height, axis=0)))
    planes.append(lax.optimization_barrier(jnp.sum(weight * normal_x, axis=0)))
    planes.append(lax.optimization_barrier(jnp.sum(weight * normal_y, axis=0)))
    planes.append(lax.optimization_barrier(jnp.sum(weight * normal_z, axis=0)))
    return jnp.stack(planes, axis=0)

def shade_image(extended, rows, cols):
    colour = extended[0:3]
    normal = extended[5:8]
    facing = jnp.maximum(light_x * normal[0] + light_y * normal[1] + light_z * normal[2], 0.0)
    lit = colour * (0.4 + 0.6 * facing)
    stacked = jnp.concatenate([extended, lit], axis=0)
    centre = extended[:, RADIUS:RADIUS + rows, RADIUS:RADIUS + cols]
    span = 2 * RADIUS + 1

    def row_step(offset_y, sums):
        numer, denom = sums
        offset_y = offset_y.astype(jnp.int32)
        rise = (offset_y - RADIUS).astype(jnp.float32)
        for offset_x in range(span):
            near = lax.dynamic_slice(stacked, (jnp.int32(0), offset_y, jnp.int32(offset_x)), (11, rows, cols))
            run = float(offset_x - RADIUS)
            exponent = -(rise * rise + run * run) * spatial_scale
            exponent = exponent - depth_weight * (centre[4] - near[4]) ** 2
            exponent = exponent - normal_weight * lax.optimization_barrier(jnp.sum((centre[5:8] - near[5:8]) ** 2, axis=0))
            weight = near[3] * jnp.exp(exponent)
            numer = numer + weight * near[8:11]
            denom = denom + weight
        return (numer, denom)
    start = (jnp.zeros((3, rows, cols), jnp.float32), jnp.zeros((rows, cols), jnp.float32))
    numer, denom = lax.fori_loop(0, span, row_step, start)
    return numer / (1.0 + denom)

def reference(density, view_flip, tf_coeff):
    padded = jnp.pad(density, ((1, 1), (1, 1), (0, 0)))

    def strip(index):
        field = lax.dynamic_slice(padded, (jnp.int32(0), index * ROWS_DEV, jnp.int32(0)), (NZ + 2, ROWS_DEV + 2, W))
        field = field.astype(jnp.float32) / 255.0
        return integrate(field, view_flip[index], tf_coeff, jnp.int32(0), NZ)
    planes = lax.map(strip, jnp.arange(N_TILE, dtype=jnp.int32))
    composited = jnp.transpose(planes, (1, 0, 2, 3)).reshape(8, H, W)
    extended = jnp.pad(composited, ((0, 0), (RADIUS, RADIUS), (RADIUS, RADIUS)))
    return shade_image(extended, H, W)
```

```python
import jax
import jax.numpy as jnp
from jax import lax
from jax.experimental import pallas as pl
from jax.experimental.pallas import tpu as pltpu
from jax.sharding import PartitionSpec as P

f32 = jnp.float32
LOG2E = 1.4426950408889634
LIGHT = (0.48, 0.6, 0.64)
RADIUS = 8
SPAN = 2 * RADIUS + 1
BANDS = 2
CHUNKS = 4


def rows_at(start, count=8):
    return pl.ds(pl.multiple_of(start, 8), count)


def poly(a, x):
    return a[0] + x * (a[1] + x * (a[2] + x * a[3]))


def level_coeffs(tf):
    s = 2.0 / 255.0
    table = []
    for q in range(4):
        c0, c1, c2, c3 = (tf[q, i] for i in range(4))
        m = LOG2E if q == 0 else 0.5
        table.append(
            (
                (c0 - c1 + c2 - c3) * m,
                (c1 - 2.0 * c2 + 3.0 * c3) * (s * m),
                (c2 - 3.0 * c3) * (s * s * m),
                c3 * (s * s * s * m),
            )
        )
    return table


def kernel(flip_ref, tf_ref, dens, out_ref, raw, fld, gxs, zh, rh, outb, mine, sibr, parts, feat, pk, hw, he, shf,
           load_sem, zs, zr, rs, rr, ss, sr, cs, cr, hs, hr):
    nd, nt = 8, 32
    d, t = lax.axis_index("depth"), lax.axis_index("tile")
    core, chip = d % 2, d // 2
    flip = flip_ref[0]
    flipped = flip == 1
    cells = dens.shape[0]
    per = cells // CHUNKS
    up_d, dn_d = (d + 1) % nd, (d + nd - 1) % nd
    up_t, dn_t = (t + 1) % nt, (t + nt - 1) % nt
    sib = 2 * chip + 1 - core

    loads = []
    for c in range(CHUNKS):
        piece = pl.ds(c * per, per)
        loads.append(pltpu.make_async_copy(dens.at[piece], raw.at[piece], load_sem.at[c]))
        loads[-1].start()

    barrier = pltpu.get_barrier_semaphore()
    near = [{"depth": up_d}, {"depth": dn_d}, {"tile": up_t}, {"tile": dn_t}]
    near += [{"depth": a, "tile": b} for a in (up_d, dn_d) for b in (up_t, dn_t)]
    near += [{"depth": (d + 2 * e) % nd} for e in (1, 2, 3)]
    for who in near:
        pl.semaphore_signal(barrier, inc=1, device_id=who, device_id_type=pl.DeviceIdType.MESH)
    pl.semaphore_wait(barrier, len(near))

    def remote(src, dst, send, recv, who):
        return pltpu.make_async_remote_copy(src_ref=src, dst_ref=dst, send_sem=send, recv_sem=recv, device_id=who,
                                            device_id_type=pl.DeviceIdType.MESH)

    edge = [
        remote(dens.at[cells - 1], zh.at[0], zs.at[0], zr.at[0], {"depth": up_d}),
        remote(dens.at[0], zh.at[1], zs.at[1], zr.at[1], {"depth": dn_d}),
        remote(dens.at[:, pl.ds(63, 1)], rh.at[0], rs.at[0], rr.at[0], {"tile": up_t}),
        remote(dens.at[:, pl.ds(0, 1)], rh.at[1], rs.at[1], rr.at[1], {"tile": dn_t}),
    ]
    for copy in edge:
        copy.start()

    lane = lax.broadcasted_iota(jnp.int32, (8, 128), 1)

    def prepare(z, carry):
        for g in range(8):
            v = [raw[z, 8 * g : 8 * g + 8, 128 * j : 128 * j + 128].astype(f32) for j in range(8)]
            zero = jnp.zeros((8, 128), f32)
            for j in range(8):
                right = v[j + 1] if j < 7 else zero
                left = v[j - 1] if j > 0 else zero
                hi = pltpu.roll(jnp.where(lane == 0, right, v[j]), 127, 1)
                lo = pltpu.roll(jnp.where(lane == 127, left, v[j]), 1, 1)
                fld[z + 1, j, 8 * g + 8 : 8 * g + 16, :] = v[j]
                gxs[z, j, 8 * g : 8 * g + 8, :] = hi - lo
        return carry

    for c in range(CHUNKS):
        loads[c].wait()
        lax.fori_loop(c * per, (c + 1) * per, prepare, 0)
    for copy in edge:
        copy.wait()

    keep = [jnp.where(d > 0, 1.0, 0.0), jnp.where(d < nd - 1, 1.0, 0.0)]
    keep_row = [jnp.where(t > 0, 1.0, 0.0), jnp.where(t < nt - 1, 1.0, 0.0)]

    def fill_planes(g, carry):
        for side, place in ((0, 0), (1, cells + 1)):
            for j in range(8):
                v = zh[side, rows_at(8 * g), 128 * j : 128 * j + 128].astype(f32)
                fld[place, j, rows_at(8 * g + 8), :] = v * keep[side]
        return carry

    lax.fori_loop(0, 8, fill_planes, 0)

    def fill_rows(z, carry):
        for side, place in ((0, 7), (1, 72)):
            for j in range(8):
                v = rh[side, z, :, 128 * j : 128 * j + 128].astype(f32)
                fld[z + 1, j, place : place + 1, :] = v * keep_row[side]
        return carry

    lax.fori_loop(0, cells, fill_rows, 0)

    a = level_coeffs(tf_ref)
    sgn = jnp.where(flipped, -1, 1)
    sf = jnp.where(flipped, -1.0, 1.0)
    z0 = jnp.where(flipped, cells + 1, 0)
    lx, ly, lz = (0.65 / 0.35 * c for c in LIGHT)
    lz = lz * sf
    order = jnp.where(flipped, nd - 1 - d, d).astype(f32)
    h0 = order * (cells / 256.0) + 0.5 / 256.0
    h1 = h0 + (cells - 1) / 256.0

    def march(j, dst, slot):
        def bands(b, carry):
            base = 8 * BANDS * b

            def cell(k, state):
                zc = z0 + sgn * (k + 1)
                new = []
                for i in range(BANDS):
                    prev, cur, S, T, sums, aw, c1, c2, c3, nx, ny, nz = state[i]
                    r0 = base + 8 * i
                    nxt = fld[zc + sgn, j, rows_at(r0 + 8), :]
                    gx = gxs[zc - 1, j, rows_at(r0), :]
                    gy = fld[zc, j, pl.ds(r0 + 9, 8), :] - fld[zc, j, pl.ds(r0 + 7, 8), :]
                    gz = nxt - prev
                    r = lax.rsqrt((gx * gx + gy * gy) + (gz * gz + 65025.0))
                    S = S + jnp.log2(1.0 + jnp.exp2(poly(a[0], cur)))
                    after = jnp.exp2(S * -0.008)
                    w = T - after
                    sums = sums + T
                    wr = w * r
                    ws = w + wr * jnp.abs(gx * lx + gy * ly + gz * lz)
                    aw = aw + ws
                    c1 = c1 + ws * jnp.tanh(poly(a[1], cur))
                    c2 = c2 + ws * jnp.tanh(poly(a[2], cur))
                    c3 = c3 + ws * jnp.tanh(poly(a[3], cur))
                    nx = nx + wr * gx
                    ny = ny + wr * gy
                    nz = nz + wr * gz
                    new.append((cur, nxt, S, after, sums, aw, c1, c2, c3, nx, ny, nz))
                return tuple(new)

            start = []
            for i in range(BANDS):
                first = fld[z0, j, rows_at(base + 8 * i + 8), :]
                zero = first * 0.0
                start.append((first, fld[z0 + sgn, j, rows_at(base + 8 * i + 8), :], zero, zero + 1.0) + (zero,) * 8)
            done = lax.fori_loop(0, cells, cell, tuple(start), unroll=16)
            for i in range(BANDS):
                _, _, _, T, sums, aw, c1, c2, c3, nx, ny, nz = done[i]
                height = (h0 - 1.0 / 256.0) + sums * (1.0 / 256.0) - T * h1
                planes = (0.175 * (aw + c1), 0.175 * (aw + c2), 0.175 * (aw + c3), T, height, nx, ny, nz * sf)
                for p in range(8):
                    dst[slot, p, rows_at(base + 8 * i), :] = planes[p]
            return carry

        lax.fori_loop(0, 8 // BANDS, bands, 0)

    own_front = core == flip

    def to_sibling(s):
        return remote(outb.at[s], sibr.at[s], ss.at[s], sr.at[s], {"depth": sib})

    def to_chip(s, e):
        return remote(mine.at[s], parts.at[(4 - e) % 4], cs.at[s], cr.at[(4 - e) % 4], {"depth": (d + 2 * e) % nd})

    def offset(s):
        return (10 - s + 3 * (s * (s - 1) // 2)) % 4

    def step(s, carry):
        e = offset(s)
        block = 2 * ((chip + e) % 4)
        march(block + 1 - core, outb, s)
        to_sibling(s).start()
        march(block + core, mine, s)
        to_sibling(s).wait_recv()

        def merge(g, c):
            rows = rows_at(8 * g)
            x = [mine[s, p, rows, :] for p in range(8)]
            y = [sibr[s, p, rows, :] for p in range(8)]
            front = [jnp.where(own_front, x[p], y[p]) for p in range(8)]
            back = [jnp.where(own_front, y[p], x[p]) for p in range(8)]
            for p in range(8):
                mine[s, p, rows, :] = front[3] * back[p] if p == 3 else front[p] + front[3] * back[p]
            return c

        lax.fori_loop(0, 8, merge, 0)

        @pl.when(s < 3)
        def _():
            to_chip(s, e).start()

        return carry

    lax.fori_loop(0, 4, step, 0)
    for s in range(3):
        to_chip(s, (2, 1, 3)[s]).wait_recv()

    kd, kn = (20.0 * LOG2E) ** 0.5, (2.0 * LOG2E) ** 0.5

    def finish(g, carry):
        rows = rows_at(8 * g)

        def part(i):
            who = jnp.where(flipped, 3 - i, i)
            slot = (who - chip + 4) % 4
            inside = slot == 0
            return [jnp.where(inside, mine[3, p, rows, :], parts[slot, p, rows, :]) for p in range(8)]

        acc = part(0)
        for i in range(1, 4):
            back = part(i)
            acc = [acc[3] * back[p] if p == 3 else acc[p] + acc[3] * back[p] for p in range(8)]
        nx, ny, nz = acc[5:8]
        facing = jnp.maximum(LIGHT[0] * nx + LIGHT[1] * ny + LIGHT[2] * nz, 0.0)
        glow = 0.4 + 0.6 * facing
        f = [acc[4] * kd, nx * kn, ny * kn, nz * kn]
        bias = jnp.log2(jnp.maximum(1.0 - acc[3], 1e-37))
        for v in f:
            bias = bias - v * v
        f += [bias] + [acc[p] * glow for p in range(3)]
        packed = pltpu.roll(f[0], 8, 1)
        for p in range(8):
            feat[p, rows_at(8 * g + 8), :] = f[p]
            if p:
                packed = jnp.where(lane >= 16 * p, pltpu.roll(f[p], 16 * p + 8 if p < 7 else 120, 1), packed)
        pk[rows, :] = packed
        return carry

    lax.fori_loop(0, 8, finish, 0)

    top, bottom = pl.ds(0, 8), pl.ds(72, 8)
    halo = [
        remote(feat.at[:, pl.ds(8, 8)], feat.at[:, bottom], hs.at[0], hr.at[0], {"tile": dn_t}),
        remote(feat.at[:, pl.ds(64, 8)], feat.at[:, top], hs.at[1], hr.at[1], {"tile": up_t}),
        remote(pk, he.at[pl.ds(8, 64)], hs.at[2], hr.at[2], {"depth": dn_d}),
        remote(pk, hw.at[pl.ds(8, 64)], hs.at[3], hr.at[3], {"depth": up_d}),
        remote(pk.at[pl.ds(0, 8)], he.at[bottom], hs.at[4], hr.at[4], {"depth": dn_d, "tile": dn_t}),
        remote(pk.at[pl.ds(56, 8)], he.at[top], hs.at[5], hr.at[5], {"depth": dn_d, "tile": up_t}),
        remote(pk.at[pl.ds(0, 8)], hw.at[bottom], hs.at[6], hr.at[6], {"depth": up_d, "tile": dn_t}),
        remote(pk.at[pl.ds(56, 8)], hw.at[top], hs.at[7], hr.at[7], {"depth": up_d, "tile": up_t}),
    ]
    for copy in halo:
        copy.start()
    for copy in halo:
        copy.wait()
    for s in range(4):
        to_sibling(s).wait_send()
    for s in range(3):
        to_chip(s, (2, 1, 3)[s]).wait_send()

    def shift_rows(i, carry):
        rows = rows_at(8 * i)
        both = jnp.where(lane % 16 < 8, hw[rows, :], he[rows, :])
        absent = ((i == 0) & (t == 0)) | ((i == 9) & (t == nt - 1))
        for p in range(8):
            x = feat[p, rows, :]
            h = pltpu.roll(both, (120 - 16 * p) % 128, 1)
            if p == 4:
                outside = jnp.where(lane < 64, jnp.where(d == nd - 1, 1, 0), jnp.where(d == 0, 1, 0))
                h = jnp.where(outside == 1, -1e30, h)
                h = jnp.where(absent, -1e30, h)
                x = jnp.where(absent, -1e30, x)
            for k in range(SPAN):
                dx = k - RADIUS
                if dx == 0:
                    y = x
                elif dx > 0:
                    y = pltpu.roll(jnp.where(lane < dx, h, x), 128 - dx, 1)
                else:
                    y = pltpu.roll(jnp.where(lane >= 128 + dx, h, x), -dx, 1)
                if p == 4:
                    y = y - dx * dx * (LOG2E / 72.0)
                shf[k, p, rows, :] = y
        return carry

    lax.fori_loop(0, 10, shift_rows, 0)

    def shade(g, carry):
        own = [feat[p, rows_at(8 * g + 8), :] for p in range(4)]
        twice = [v * 2.0 for v in own]
        zero = own[0] * 0.0

        def line(dy, sums):
            rows = pl.ds(8 * g + dy, 8)
            part = [None] * 4
            for k in range(SPAN):
                e = shf[k, 4, rows, :]
                for p in range(4):
                    e = e + twice[p] * shf[k, p, rows, :]
                w = jnp.exp2(e)
                for c in range(3):
                    term = w * shf[k, 5 + c, rows, :]
                    part[c] = term if k == 0 else part[c] + term
                part[3] = w if k == 0 else part[3] + w
            rise = (dy - RADIUS).astype(f32)
            fall = jnp.exp2(zero + rise * rise * (-LOG2E / 72.0))
            return tuple(sums[c] + fall * part[c] for c in range(4))

        sums = lax.fori_loop(0, SPAN, line, (zero,) * 4)
        norm = own[0] * own[0]
        for v in own[1:]:
            norm = norm + v * v
        scale = jnp.exp2(-norm)
        inv = scale / (1.0 + scale * sums[3])
        for c in range(3):
            out_ref[c, rows_at(8 * g), :] = sums[c] * inv
        return carry

    lax.fori_loop(0, 8, shade, 0)


def per_device(density, view_flip, tf_coeff):
    i32 = jnp.int32
    dma = pltpu.SemaphoreType.DMA
    image = (8, 64, 128)
    return pl.pallas_call(
        kernel,
        out_shape=jax.ShapeDtypeStruct((3, 64, 128), f32),
        in_specs=[
            pl.BlockSpec(memory_space=pltpu.SMEM),
            pl.BlockSpec(memory_space=pltpu.SMEM),
            pl.BlockSpec(memory_space=pl.ANY),
        ],
        out_specs=pl.BlockSpec(memory_space=pltpu.VMEM),
        scratch_shapes=[
            pltpu.VMEM((32, 64, 1024), i32),
            pltpu.VMEM((34, 8, 80, 128), f32),
            pltpu.VMEM((32, 8, 64, 128), f32),
            pltpu.VMEM((2, 64, 1024), i32),
            pltpu.VMEM((2, 32, 1, 1024), i32),
            pltpu.VMEM((4,) + image, f32),
            pltpu.VMEM((4,) + image, f32),
            pltpu.VMEM((4,) + image, f32),
            pltpu.VMEM((4,) + image, f32),
            pltpu.VMEM((8, 80, 128), f32),
            pltpu.VMEM((64, 128), f32),
            pltpu.VMEM((80, 128), f32),
            pltpu.VMEM((80, 128), f32),
            pltpu.VMEM((SPAN, 8, 80, 128), f32),
            dma((CHUNKS,)),
            dma((2,)), dma((2,)),
            dma((2,)), dma((2,)),
            dma((4,)), dma((4,)),
            dma((4,)), dma((4,)),
            dma((8,)), dma((8,)),
        ],
        compiler_params=pltpu.CompilerParams(
            collective_id=0, has_side_effects=True, vmem_limit_bytes=60 * 1024 * 1024
        ),
        name="render",
    )(view_flip, tf_coeff, density)


def solution(mesh):
    in_specs = (P("depth", "tile", None), P("tile"), P())
    out_specs = P(None, "tile", "depth")
    return jax.shard_map(per_device, mesh=mesh, in_specs=in_specs, out_specs=out_specs, check_vma=False)
```

```python
import jax
import jax.numpy as jnp
from jax import lax
from jax.experimental import pallas as pl
from jax.experimental.pallas import tpu as pltpu
from jax.sharding import PartitionSpec as P

f32 = jnp.float32
LOG2E = 1.4426950408889634
LIGHT = (0.48, 0.6, 0.64)
RADIUS = 8
SPAN = 2 * RADIUS + 1
BANDS = 2


def rows_at(start, count=8):
    return pl.ds(pl.multiple_of(start, 8), count)


def poly(a, x):
    return a[0] + x * (a[1] + x * (a[2] + x * a[3]))


def level_coeffs(tf):
    s = 2.0 / 255.0
    table = []
    for q in range(4):
        c0, c1, c2, c3 = (tf[q, i] for i in range(4))
        m = LOG2E if q == 0 else 0.5
        table.append(
            (
                (c0 - c1 + c2 - c3) * m,
                (c1 - 2.0 * c2 + 3.0 * c3) * (s * m),
                (c2 - 3.0 * c3) * (s * s * m),
                c3 * (s * s * s * m),
            )
        )
    return table


def kernel(flip_ref, tf_ref, dens, out_ref, raw, fld, zh, rh, inner, image, sibr, parts, feat, pk, hw, he, rim, shf, tot,
           load_sem, zs, zr, rs, rr, ss, sr, cs, cr, hs, hr):
    nd, nt = 8, 32
    d, t = lax.axis_index("depth"), lax.axis_index("tile")
    core, chip = d % 2, d // 2
    flip = flip_ref[0]
    flipped = flip == 1
    cells = dens.shape[0]
    up_d, dn_d = (d + 1) % nd, (d + nd - 1) % nd
    up_t, dn_t = (t + 1) % nt, (t + nt - 1) % nt
    sib = 2 * chip + 1 - core

    def load(i):
        j = (2 * ((chip + 2) % 4) + 7 + i) % 8
        piece = dens.at[:, :, pl.ds(pl.multiple_of(128 * j, 128), 128)]
        return j, pltpu.make_async_copy(piece, raw.at[j], load_sem.at[i])

    for i in range(8):
        load(i)[1].start()

    barrier = pltpu.get_barrier_semaphore()
    near = [{"depth": up_d}, {"depth": dn_d}, {"tile": up_t}, {"tile": dn_t}]
    near += [{"depth": a, "tile": b} for a in (up_d, dn_d) for b in (up_t, dn_t)]
    near += [{"depth": (d + 2 * e) % nd} for e in (1, 2, 3)]
    for who in near:
        pl.semaphore_signal(barrier, inc=1, device_id=who, device_id_type=pl.DeviceIdType.MESH)

    def clear(z, carry):
        for j in (0, 9):
            for g in range(8):
                fld[z + 1, j, 8 * g + 8 : 8 * g + 16, :] = jnp.zeros((8, 128), f32)
        return carry

    lax.fori_loop(0, cells, clear, 0)
    pl.semaphore_wait(barrier, len(near))

    def remote(src, dst, send, recv, who):
        return pltpu.make_async_remote_copy(src_ref=src, dst_ref=dst, send_sem=send, recv_sem=recv, device_id=who,
                                            device_id_type=pl.DeviceIdType.MESH)

    edge = [
        remote(dens.at[cells - 1], zh.at[0], zs.at[0], zr.at[0], {"depth": up_d}),
        remote(dens.at[0], zh.at[1], zs.at[1], zr.at[1], {"depth": dn_d}),
        remote(dens.at[:, pl.ds(63, 1)], rh.at[0], rs.at[0], rr.at[0], {"tile": up_t}),
        remote(dens.at[:, pl.ds(0, 1)], rh.at[1], rs.at[1], rr.at[1], {"tile": dn_t}),
    ]
    for copy in edge:
        copy.start()

    lane = lax.broadcasted_iota(jnp.int32, (8, 128), 1)
    first_lane, last_lane = lane == 0, lane == 127
    a = level_coeffs(tf_ref)
    sgn = jnp.where(flipped, -1, 1)
    sf = jnp.where(flipped, -1.0, 1.0)
    z0 = jnp.where(flipped, cells + 1, 0)
    lx, ly, lz = (0.65 / 0.35 * c for c in LIGHT)
    lz = lz * sf
    order = jnp.where(flipped, nd - 1 - d, d).astype(f32)
    h0 = order * (cells / 256.0) + 0.5 / 256.0
    h1 = h0 + (cells - 1) / 256.0

    def place(b, i):
        return 8 * ((BANDS * b + 1 + i) % 8)

    def cell(j, b):
        def body(k, state):
            zc = z0 + sgn * (k + 1)
            new = []
            for i in range(BANDS):
                prev, cur, S, T, sums, aw, c1, c2, c3, nx, ny, nz = state[i]
                r0 = place(b, i)
                rows = rows_at(r0 + 8)
                nxt = fld[zc + sgn, j, rows, :]
                right, left = fld[zc, j + 1, rows, :], fld[zc, j - 1, rows, :]
                ahead = pltpu.roll(jnp.where(first_lane, right, cur), 127, 1)
                behind = pltpu.roll(jnp.where(last_lane, left, cur), 1, 1)
                gx = ahead - behind
                gy = fld[zc, j, pl.ds(r0 + 9, 8), :] - fld[zc, j, pl.ds(r0 + 7, 8), :]
                gz = nxt - prev
                r = lax.rsqrt((gx * gx + gy * gy) + (gz * gz + 65025.0))
                S = S + jnp.log2(1.0 + jnp.exp2(poly(a[0], cur)))
                after = jnp.exp2(S * -0.008)
                w = T - after
                sums = sums + T
                wr = w * r
                ws = w + wr * jnp.abs(gx * lx + gy * ly + gz * lz)
                aw = aw + ws
                c1 = c1 + ws * jnp.tanh(poly(a[1], cur))
                c2 = c2 + ws * jnp.tanh(poly(a[2], cur))
                c3 = c3 + ws * jnp.tanh(poly(a[3], cur))
                nx = nx + wr * gx
                ny = ny + wr * gy
                nz = nz + wr * gz
                new.append((cur, nxt, S, after, sums, aw, c1, c2, c3, nx, ny, nz))
            return tuple(new)

        return body

    def enter(j, b, k):
        start = []
        for i in range(BANDS):
            rows = rows_at(place(b, i) + 8)
            prev, cur = fld[z0 + sgn * k, j, rows, :], fld[z0 + sgn * (k + 1), j, rows, :]
            zero = cur * 0.0
            start.append((prev, cur, zero, zero + 1.0) + (zero,) * 8)
        return tuple(start)

    def leave(state, b, slot):
        for i in range(BANDS):
            _, _, _, T, sums, aw, c1, c2, c3, nx, ny, nz = state[i]
            height = (h0 - 1.0 / 256.0) + sums * (1.0 / 256.0) - T * h1
            planes = (0.175 * (aw + c1), 0.175 * (aw + c2), 0.175 * (aw + c3), T, height, nx, ny, nz * sf)
            for p in range(8):
                image[slot, p, rows_at(place(b, i)), :] = planes[p]

    def offset(s):
        return (10 - s + 3 * (s * (s - 1) // 2)) % 4

    def block_of(h):
        return 2 * ((chip + offset(h // 2)) % 4) + (h + core + 1) % 2 + 1

    def take(i, carry):
        j, copy = load(i)
        copy.wait()

        def layer(z, c):
            for g in range(8):
                fld[z + 1, j + 1, 8 * g + 8 : 8 * g + 16, :] = raw[j, z, 8 * g : 8 * g + 8, :].astype(f32)
            return c

        return lax.fori_loop(0, cells, layer, carry, unroll=2)

    lax.fori_loop(0, 4, take, 0)

    def early(n, carry):
        h, b = n // 3, n % 3
        j = block_of(h)
        done = lax.fori_loop(1, cells - 1, cell(j, b), enter(j, b, 1), unroll=15)
        for i in range(BANDS):
            for q, v in enumerate(done[i][2:3] + done[i][4:]):
                inner[h, q, rows_at(place(b, i)), :] = v
        return carry

    lax.fori_loop(0, 6, early, 0)
    lax.fori_loop(4, 8, take, 0)
    for copy in edge:
        copy.wait()

    keep = [jnp.where(d > 0, 1.0, 0.0), jnp.where(d < nd - 1, 1.0, 0.0)]
    keep_row = [jnp.where(t > 0, 1.0, 0.0), jnp.where(t < nt - 1, 1.0, 0.0)]

    def fill_planes(g, carry):
        for side, layer in ((0, 0), (1, cells + 1)):
            for j in range(8):
                v = zh[side, rows_at(8 * g), 128 * j : 128 * j + 128].astype(f32)
                fld[layer, j + 1, rows_at(8 * g + 8), :] = v * keep[side]
        return carry

    lax.fori_loop(0, 8, fill_planes, 0)

    def fill_rows(z, carry):
        for side, row in ((0, 7), (1, 72)):
            for j in range(8):
                v = rh[side, z, :, 128 * j : 128 * j + 128].astype(f32)
                fld[z + 1, j + 1, row : row + 1, :] = v * keep_row[side]
        return carry

    lax.fori_loop(0, cells, fill_rows, 0)

    own_front = core == flip

    def to_sibling(s):
        return remote(image.at[2 * s], sibr.at[s], ss.at[s], sr.at[s], {"depth": sib})

    def to_chip(s, e):
        return remote(image.at[2 * s + 1], parts.at[(4 - e) % 4], cs.at[s], cr.at[(4 - e) % 4],
                      {"depth": (d + 2 * e) % nd})

    def half_step(h, carry):
        j = block_of(h)
        s = h // 2

        def bands(b, c):
            resumed = (h < 2) & (b < 3)

            @pl.when(resumed)
            def _():
                body = cell(j, b)
                state = body(0, enter(j, b, 0))
                mixed = []
                for i in range(BANDS):
                    _, _, S, T, *sums = state[i]
                    rows = rows_at(place(b, i))
                    mid = [inner[h, q, rows, :] for q in range(9)]
                    S = S + mid[0]
                    sums = [v + T * m for v, m in zip(sums, mid[1:])]
                    tail = rows_at(place(b, i) + 8)
                    prev, cur = fld[z0 + sgn * (cells - 1), j, tail, :], fld[z0 + sgn * cells, j, tail, :]
                    mixed.append((prev, cur, S, jnp.exp2(S * -0.008), *sums))
                leave(body(cells - 1, tuple(mixed)), b, h)

            @pl.when(jnp.logical_not(resumed))
            def _():
                leave(lax.fori_loop(0, cells, cell(j, b), enter(j, b, 0), unroll=16), b, h)

            return c

        lax.fori_loop(0, 8 // BANDS, bands, 0)

        @pl.when(h % 2 == 0)
        def _():
            to_sibling(s).start()

        @pl.when(h % 2 == 1)
        def _():
            to_sibling(s).wait_recv()

            def merge(g, c):
                rows = rows_at(8 * g)
                x = [image[h, p, rows, :] for p in range(8)]
                y = [sibr[s, p, rows, :] for p in range(8)]
                front = [jnp.where(own_front, x[p], y[p]) for p in range(8)]
                back = [jnp.where(own_front, y[p], x[p]) for p in range(8)]
                for p in range(8):
                    image[h, p, rows, :] = front[3] * back[p] if p == 3 else front[p] + front[3] * back[p]
                return c

            lax.fori_loop(0, 8, merge, 0)

            @pl.when(s < 3)
            def _():
                to_chip(s, offset(s)).start()

        return carry

    lax.fori_loop(0, 8, half_step, 0)
    for s in range(3):
        to_chip(s, (2, 1, 3)[s]).wait_recv()

    kd, kn = (20.0 * LOG2E) ** 0.5, (2.0 * LOG2E) ** 0.5

    def finish(g, carry):
        rows = rows_at(8 * g)

        def part(i):
            who = jnp.where(flipped, 3 - i, i)
            slot = (who - chip + 4) % 4
            inside = slot == 0
            return [jnp.where(inside, image[7, p, rows, :], parts[slot, p, rows, :]) for p in range(8)]

        acc = part(0)
        for i in range(1, 4):
            back = part(i)
            acc = [acc[3] * back[p] if p == 3 else acc[p] + acc[3] * back[p] for p in range(8)]
        nx, ny, nz = acc[5:8]
        facing = jnp.maximum(LIGHT[0] * nx + LIGHT[1] * ny + LIGHT[2] * nz, 0.0)
        glow = 0.4 + 0.6 * facing
        f = [acc[4] * kd, nx * kn, ny * kn, nz * kn]
        bias = jnp.log2(jnp.maximum(1.0 - acc[3], 1e-37))
        for v in f:
            bias = bias - v * v
        f += [bias] + [acc[p] * glow for p in range(3)]
        packed = pltpu.roll(f[0], 8, 1)
        for p in range(8):
            feat[p, rows_at(8 * g + 8), :] = f[p]
            if p:
                packed = jnp.where(lane >= 16 * p, pltpu.roll(f[p], 16 * p + 8, 1), packed)
        pk[rows, :] = packed
        return carry

    lax.fori_loop(0, 8, finish, 0)

    top, bottom = pl.ds(0, 8), pl.ds(72, 8)
    halo = [
        remote(feat.at[:, pl.ds(8, 8)], feat.at[:, bottom], hs.at[0], hr.at[0], {"tile": dn_t}),
        remote(feat.at[:, pl.ds(64, 8)], feat.at[:, top], hs.at[1], hr.at[1], {"tile": up_t}),
        remote(pk, he.at[pl.ds(8, 64)], hs.at[2], hr.at[2], {"depth": dn_d}),
        remote(pk, hw.at[pl.ds(8, 64)], hs.at[3], hr.at[3], {"depth": up_d}),
        remote(pk.at[pl.ds(0, 8)], he.at[bottom], hs.at[4], hr.at[4], {"depth": dn_d, "tile": dn_t}),
        remote(pk.at[pl.ds(56, 8)], he.at[top], hs.at[5], hr.at[5], {"depth": dn_d, "tile": up_t}),
        remote(pk.at[pl.ds(0, 8)], hw.at[bottom], hs.at[6], hr.at[6], {"depth": up_d, "tile": dn_t}),
        remote(pk.at[pl.ds(56, 8)], hw.at[top], hs.at[7], hr.at[7], {"depth": up_d, "tile": up_t}),
    ]
    for copy in halo:
        copy.start()

    def shift_rows(i, carry):
        rows = rows_at(8 * i)
        for p in range(8):
            x = feat[p, rows, :]
            for k in range(SPAN):
                dx = k - RADIUS
                y = pltpu.roll(x, (-dx) % 128, 1) if dx else x
                if p == 4:
                    y = y - dx * dx * (LOG2E / 72.0)
                    if dx:
                        y = jnp.where(lane >= 128 - dx if dx > 0 else lane < -dx, -1e30, y)
                shf[k, p, rows, :] = y
        return carry

    def fall(dy, like):
        rise = (dy - RADIUS).astype(f32)
        return jnp.exp2(like * 0.0 + rise * rise * (-LOG2E / 72.0))

    def add_tap(part, q, twice):
        e = q[4]
        for p in range(4):
            e = e + twice[p] * q[p]
        w = jnp.exp2(e)
        terms = [w * q[5], w * q[6], w * q[7], w]
        return terms if part is None else [u + v for u, v in zip(part, terms)]

    def inside(g, carry):
        twice = [feat[p, rows_at(8 * g + 8), :] * 2.0 for p in range(4)]

        def line(dy, sums):
            rows = pl.ds(8 * g + dy, 8)
            part = None
            for k in range(SPAN):
                part = add_tap(part, [shf[k, p, rows, :] for p in range(8)], twice)
            f = fall(dy, twice[0])
            return tuple(u + f * v for u, v in zip(sums, part))

        sums = lax.fori_loop(0, SPAN, line, (twice[0] * 0.0,) * 4, unroll=4)
        for c in range(4):
            tot[c, rows_at(8 * g), :] = sums[c]
        return carry

    lax.fori_loop(1, 9, shift_rows, 0)
    lax.fori_loop(1, 7, inside, 0)
    for copy in halo:
        copy.wait()

    def absent(i):
        return ((i == 0) & (t == 0)) | ((i == 9) & (t == nt - 1))

    def outer_rows(n, carry):
        i = 9 * n
        rows = rows_at(8 * i)
        feat[4, rows, :] = jnp.where(absent(i), -1e30, feat[4, rows, :])
        shift_rows(i, 0)
        return inside(7 * n, carry)

    lax.fori_loop(0, 2, outer_rows, 0)

    e, m = lane // 8, lane % 8
    left = e < 8
    column = e + m
    there = jnp.where(left, jnp.where(column <= 7, 1, 0), jnp.where(column >= 15, 1, 0))
    there = there * jnp.where(left, jnp.where(d > 0, 1, 0), jnp.where(d < nd - 1, 1, 0))
    source = jnp.where(left, column % 8, 8 + (column + 1) % 8)
    run = jnp.where(left, 8 - m, m + 1).astype(f32)
    drop = jnp.where(there == 1, run * run * (-LOG2E / 72.0), -1e30)
    pixel = jnp.where(left, e, 112 + e)
    home = jnp.where(lane < 8, 8 * lane, jnp.where(lane >= 120, 8 * (lane - 112), 0))
    edge_lane = (lane < 8) | (lane >= 120)

    def rim_rows(i, carry):
        rows = rows_at(8 * i)
        both = jnp.where(lane % 16 < 8, hw[rows, :], he[rows, :])
        for p in range(8):
            v = jnp.take_along_axis(both, source + 16 * p, axis=1)
            if p == 4:
                v = jnp.where(absent(i), -1e30, v + drop)
            rim[p, rows, :] = v
        return carry

    lax.fori_loop(0, 10, rim_rows, 0)

    def outside(g, carry):
        own = [feat[p, rows_at(8 * g + 8), :] for p in range(4)]
        twice = [jnp.take_along_axis(v * 2.0, pixel, axis=1) for v in own]

        def line(dy, sums):
            part = add_tap(None, [rim[p, pl.ds(8 * g + dy, 8), :] for p in range(8)], twice)
            f = fall(dy, twice[0])
            return tuple(u + f * v for u, v in zip(sums, part))

        sums = lax.fori_loop(0, SPAN, line, (twice[0] * 0.0,) * 4, unroll=17)
        total = []
        for c in range(4):
            v = sums[c]
            for step in (1, 2, 4):
                v = v + pltpu.roll(v, 128 - step, 1)
            v = jnp.take_along_axis(v, home, axis=1)
            total.append(tot[c, rows_at(8 * g), :] + jnp.where(edge_lane, v, 0.0))
        norm = own[0] * own[0]
        for v in own[1:]:
            norm = norm + v * v
        scale = jnp.exp2(-norm)
        inv = scale / (1.0 + scale * total[3])
        for c in range(3):
            out_ref[c, rows_at(8 * g), :] = total[c] * inv
        return carry

    lax.fori_loop(0, 8, outside, 0)
    for s in range(4):
        to_sibling(s).wait_send()
    for s in range(3):
        to_chip(s, (2, 1, 3)[s]).wait_send()


def per_device(density, view_flip, tf_coeff):
    i32 = jnp.int32
    dma = pltpu.SemaphoreType.DMA
    image = (8, 64, 128)
    return pl.pallas_call(
        kernel,
        out_shape=jax.ShapeDtypeStruct((3, 64, 128), f32),
        in_specs=[
            pl.BlockSpec(memory_space=pltpu.SMEM),
            pl.BlockSpec(memory_space=pltpu.SMEM),
            pl.BlockSpec(memory_space=pl.ANY),
        ],
        out_specs=pl.BlockSpec(memory_space=pltpu.VMEM),
        scratch_shapes=[
            pltpu.VMEM((8, 32, 64, 128), i32),
            pltpu.VMEM((34, 10, 80, 128), f32),
            pltpu.VMEM((2, 64, 1024), i32),
            pltpu.VMEM((2, 32, 1, 1024), i32),
            pltpu.VMEM((2, 9, 64, 128), f32),
            pltpu.VMEM((8,) + image, f32),
            pltpu.VMEM((4,) + image, f32),
            pltpu.VMEM((4,) + image, f32),
            pltpu.VMEM((8, 80, 128), f32),
            pltpu.VMEM((64, 128), f32),
            pltpu.VMEM((80, 128), f32),
            pltpu.VMEM((80, 128), f32),
            pltpu.VMEM((8, 80, 128), f32),
            pltpu.VMEM((SPAN, 8, 80, 128), f32),
            pltpu.VMEM((4, 64, 128), f32),
            dma((8,)),
            dma((2,)), dma((2,)),
            dma((2,)), dma((2,)),
            dma((4,)), dma((4,)),
            dma((4,)), dma((4,)),
            dma((8,)), dma((8,)),
        ],
        compiler_params=pltpu.CompilerParams(
            collective_id=0, has_side_effects=True, vmem_limit_bytes=60 * 1024 * 1024
        ),
        name="render",
    )(view_flip, tf_coeff, density)


def solution(mesh):
    in_specs = (P("depth", "tile", None), P("tile"), P())
    out_specs = P(None, "tile", "depth")
    return jax.shard_map(per_device, mesh=mesh, in_specs=in_specs, out_specs=out_specs, check_vma=False)
```

```python
import jax
import jax.numpy as jnp
from jax import lax
from jax.experimental import pallas as pl
from jax.experimental.pallas import tpu as pltpu
from jax.sharding import PartitionSpec as P

f32 = jnp.float32
LOG2E = 1.4426950408889634
LIGHT = (0.48, 0.6, 0.64)
RADIUS = 8
SPAN = 2 * RADIUS + 1
BANDS = 2


def rows_at(start, count=8):
    return pl.ds(pl.multiple_of(start, 8), count)


def poly(a, x):
    return a[0] + x * (a[1] + x * (a[2] + x * a[3]))


def level_coeffs(tf):
    s = 2.0 / 255.0
    table = []
    for q in range(4):
        c0, c1, c2, c3 = (tf[q, i] for i in range(4))
        m = LOG2E if q == 0 else 0.5
        table.append(
            (
                (c0 - c1 + c2 - c3) * m,
                (c1 - 2.0 * c2 + 3.0 * c3) * (s * m),
                (c2 - 3.0 * c3) * (s * s * m),
                c3 * (s * s * s * m),
            )
        )
    return table


def kernel(flip_ref, tf_ref, dens, out_ref, raw, fld, zh, rh, inner, image, sibr, parts, feat, pk, hw, he, rim, shf, tot,
           load_sem, zs, zr, rs, rr, ss, sr, cs, cr, hs, hr):
    nd, nt = 8, 32
    d, t = lax.axis_index("depth"), lax.axis_index("tile")
    core, chip = d % 2, d // 2
    flip = flip_ref[0]
    flipped = flip == 1
    cells = dens.shape[0]
    up_d, dn_d = (d + 1) % nd, (d + nd - 1) % nd
    up_t, dn_t = (t + 1) % nt, (t + nt - 1) % nt
    sib = 2 * chip + 1 - core

    def load(i):
        j = (2 * ((chip + 2) % 4) + 7 + i) % 8
        piece = dens.at[:, :, pl.ds(pl.multiple_of(128 * j, 128), 128)]
        return j, pltpu.make_async_copy(piece, raw.at[j], load_sem.at[i])

    for i in range(8):
        load(i)[1].start()

    barrier = pltpu.get_barrier_semaphore()
    near = [{"depth": up_d}, {"depth": dn_d}, {"tile": up_t}, {"tile": dn_t}]
    near += [{"depth": a, "tile": b} for a in (up_d, dn_d) for b in (up_t, dn_t)]
    near += [{"depth": (d + 2 * e) % nd} for e in (1, 2, 3)]
    for who in near:
        pl.semaphore_signal(barrier, inc=1, device_id=who, device_id_type=pl.DeviceIdType.MESH)

    def clear(z, carry):
        for j in (0, 9):
            for g in range(8):
                fld[z + 1, j, 8 * g + 8 : 8 * g + 16, :] = jnp.zeros((8, 128), f32)
        return carry

    lax.fori_loop(0, cells, clear, 0)
    pl.semaphore_wait(barrier, len(near))

    def remote(src, dst, send, recv, who):
        return pltpu.make_async_remote_copy(src_ref=src, dst_ref=dst, send_sem=send, recv_sem=recv, device_id=who,
                                            device_id_type=pl.DeviceIdType.MESH)

    edge = [
        remote(dens.at[cells - 1], zh.at[0], zs.at[0], zr.at[0], {"depth": up_d}),
        remote(dens.at[0], zh.at[1], zs.at[1], zr.at[1], {"depth": dn_d}),
        remote(dens.at[:, pl.ds(63, 1)], rh.at[0], rs.at[0], rr.at[0], {"tile": up_t}),
        remote(dens.at[:, pl.ds(0, 1)], rh.at[1], rs.at[1], rr.at[1], {"tile": dn_t}),
    ]
    for copy in edge:
        copy.start()

    lane = lax.broadcasted_iota(jnp.int32, (8, 128), 1)
    first_lane, last_lane = lane == 0, lane == 127
    a = level_coeffs(tf_ref)
    sgn = jnp.where(flipped, -1, 1)
    sf = jnp.where(flipped, -1.0, 1.0)
    z0 = jnp.where(flipped, cells + 1, 0)
    lx, ly, lz = (0.65 / 0.35 * c for c in LIGHT)
    lz = lz * sf
    order = jnp.where(flipped, nd - 1 - d, d).astype(f32)
    h0 = order * (cells / 256.0) + 0.5 / 256.0
    h1 = h0 + (cells - 1) / 256.0

    def place(b, i):
        return 8 * ((BANDS * b + 1 + i) % 8)

    def cell(j, b):
        def body(k, state):
            zc = z0 + sgn * (k + 1)
            new = []
            for i in range(BANDS):
                prev, cur, S, T, sums, aw, c1, c2, c3, nx, ny, nl = state[i]
                r0 = place(b, i)
                rows = rows_at(r0 + 8)
                nxt = fld[zc + sgn, j, rows, :]
                right, left = fld[zc, j + 1, rows, :], fld[zc, j - 1, rows, :]
                ahead = pltpu.roll(jnp.where(first_lane, right, cur), 127, 1)
                behind = pltpu.roll(jnp.where(last_lane, left, cur), 1, 1)
                gx = ahead - behind
                gy = fld[zc, j, pl.ds(r0 + 9, 8), :] - fld[zc, j, pl.ds(r0 + 7, 8), :]
                gz = nxt - prev
                r = lax.rsqrt((gx * gx + gy * gy) + (gz * gz + 65025.0))
                S = S + jnp.log2(1.0 + jnp.exp2(poly(a[0], cur)))
                after = jnp.exp2(S * -0.008)
                w = T - after
                sums = sums + T
                wr = w * r
                lit = wr * (gx * lx + gy * ly + gz * lz)
                ws = w + jnp.abs(lit)
                aw = aw + ws
                c1 = c1 + ws * jnp.tanh(poly(a[1], cur))
                c2 = c2 + ws * jnp.tanh(poly(a[2], cur))
                c3 = c3 + ws * jnp.tanh(poly(a[3], cur))
                nx = nx + wr * gx
                ny = ny + wr * gy
                nl = nl + lit
                new.append((cur, nxt, S, after, sums, aw, c1, c2, c3, nx, ny, nl))
            return tuple(new)

        return body

    def enter(j, b, k):
        start = []
        for i in range(BANDS):
            rows = rows_at(place(b, i) + 8)
            prev, cur = fld[z0 + sgn * k, j, rows, :], fld[z0 + sgn * (k + 1), j, rows, :]
            zero = cur * 0.0
            start.append((prev, cur, zero, zero + 1.0) + (zero,) * 8)
        return tuple(start)

    def leave(state, b, slot):
        for i in range(BANDS):
            _, _, _, T, sums, aw, c1, c2, c3, nx, ny, nl = state[i]
            nz = (nl - lx * nx - ly * ny) * (0.35 / 0.65 / LIGHT[2])
            height = (h0 - 1.0 / 256.0) + sums * (1.0 / 256.0) - T * h1
            planes = (0.175 * (aw + c1), 0.175 * (aw + c2), 0.175 * (aw + c3), T, height, nx, ny, nz)
            for p in range(8):
                image[slot, p, rows_at(place(b, i)), :] = planes[p]

    def offset(s):
        return (10 - s + 3 * (s * (s - 1) // 2)) % 4

    def block_of(h):
        return 2 * ((chip + offset(h // 2)) % 4) + (h + core + 1) % 2 + 1

    def take(i, carry):
        j, copy = load(i)
        copy.wait()

        def layer(z, c):
            for g in range(8):
                fld[z + 1, j + 1, 8 * g + 8 : 8 * g + 16, :] = raw[j, z, 8 * g : 8 * g + 8, :].astype(f32)
            return c

        return lax.fori_loop(0, cells, layer, carry, unroll=2)

    lax.fori_loop(0, 4, take, 0)

    def early(n, carry):
        h, b = n // 3, n % 3
        j = block_of(h)
        done = lax.fori_loop(1, cells - 1, cell(j, b), enter(j, b, 1), unroll=30)
        for i in range(BANDS):
            for q, v in enumerate(done[i][2:3] + done[i][4:]):
                inner[h, q, rows_at(place(b, i)), :] = v
        return carry

    lax.fori_loop(0, 6, early, 0)
    lax.fori_loop(4, 8, take, 0)
    for copy in edge:
        copy.wait()

    keep = [jnp.where(d > 0, 1.0, 0.0), jnp.where(d < nd - 1, 1.0, 0.0)]
    keep_row = [jnp.where(t > 0, 1.0, 0.0), jnp.where(t < nt - 1, 1.0, 0.0)]

    def fill_planes(g, carry):
        for side, layer in ((0, 0), (1, cells + 1)):
            for j in range(8):
                v = zh[side, rows_at(8 * g), 128 * j : 128 * j + 128].astype(f32)
                fld[layer, j + 1, rows_at(8 * g + 8), :] = v * keep[side]
        return carry

    lax.fori_loop(0, 8, fill_planes, 0)

    def fill_rows(z, carry):
        for side, row in ((0, 7), (1, 72)):
            for j in range(8):
                v = rh[side, z, :, 128 * j : 128 * j + 128].astype(f32)
                fld[z + 1, j + 1, row : row + 1, :] = v * keep_row[side]
        return carry

    lax.fori_loop(0, cells, fill_rows, 0, unroll=2)

    own_front = core == flip

    def to_sibling(s):
        return remote(image.at[2 * s], sibr.at[s], ss.at[s], sr.at[s], {"depth": sib})

    def to_chip(s, e):
        return remote(image.at[2 * s + 1], parts.at[(4 - e) % 4], cs.at[s], cr.at[(4 - e) % 4],
                      {"depth": (d + 2 * e) % nd})

    def half_step(h, carry):
        j = block_of(h)
        s = h // 2

        def bands(b, c):
            resumed = (h < 2) & (b < 3)

            @pl.when(resumed)
            def _():
                body = cell(j, b)
                state = body(0, enter(j, b, 0))
                mixed = []
                for i in range(BANDS):
                    _, _, S, T, *sums = state[i]
                    rows = rows_at(place(b, i))
                    mid = [inner[h, q, rows, :] for q in range(9)]
                    S = S + mid[0]
                    sums = [v + T * m for v, m in zip(sums, mid[1:])]
                    tail = rows_at(place(b, i) + 8)
                    prev, cur = fld[z0 + sgn * (cells - 1), j, tail, :], fld[z0 + sgn * cells, j, tail, :]
                    mixed.append((prev, cur, S, jnp.exp2(S * -0.008), *sums))
                leave(body(cells - 1, tuple(mixed)), b, h)

            @pl.when(jnp.logical_not(resumed))
            def _():
                leave(lax.fori_loop(0, cells, cell(j, b), enter(j, b, 0), unroll=32), b, h)

            return c

        lax.fori_loop(0, 8 // BANDS, bands, 0)

        @pl.when(h % 2 == 0)
        def _():
            to_sibling(s).start()

        @pl.when(h % 2 == 1)
        def _():
            to_sibling(s).wait_recv()

            def merge(g, c):
                rows = rows_at(8 * g)
                x = [image[h, p, rows, :] for p in range(8)]
                y = [sibr[s, p, rows, :] for p in range(8)]
                front = [jnp.where(own_front, x[p], y[p]) for p in range(8)]
                back = [jnp.where(own_front, y[p], x[p]) for p in range(8)]
                for p in range(8):
                    image[h, p, rows, :] = front[3] * back[p] if p == 3 else front[p] + front[3] * back[p]
                return c

            lax.fori_loop(0, 8, merge, 0, unroll=2)

            @pl.when(s < 3)
            def _():
                to_chip(s, offset(s)).start()

        return carry

    lax.fori_loop(0, 8, half_step, 0)
    for s in range(3):
        to_chip(s, (2, 1, 3)[s]).wait_recv()

    kd, kn = (20.0 * LOG2E) ** 0.5, (2.0 * LOG2E) ** 0.5

    def finish(g, carry):
        rows = rows_at(8 * g)

        def part(i):
            who = jnp.where(flipped, 3 - i, i)
            slot = (who - chip + 4) % 4
            inside = slot == 0
            return [jnp.where(inside, image[7, p, rows, :], parts[slot, p, rows, :]) for p in range(8)]

        acc = part(0)
        for i in range(1, 4):
            back = part(i)
            acc = [acc[3] * back[p] if p == 3 else acc[p] + acc[3] * back[p] for p in range(8)]
        nx, ny, nz = acc[5:8]
        facing = jnp.maximum(LIGHT[0] * nx + LIGHT[1] * ny + LIGHT[2] * nz, 0.0)
        glow = 0.4 + 0.6 * facing
        f = [acc[4] * kd, nx * kn, ny * kn, nz * kn]
        bias = jnp.log2(jnp.maximum(1.0 - acc[3], 1e-37))
        for v in f:
            bias = bias - v * v
        f += [bias] + [acc[p] * glow for p in range(3)]
        packed = pltpu.roll(f[0], 8, 1)
        for p in range(8):
            feat[p, rows_at(8 * g + 8), :] = f[p]
            if p:
                packed = jnp.where(lane >= 16 * p, pltpu.roll(f[p], 16 * p + 8, 1), packed)
        pk[rows, :] = packed
        return carry

    lax.fori_loop(0, 8, finish, 0, unroll=2)

    top, bottom = pl.ds(0, 8), pl.ds(72, 8)
    halo = [
        remote(feat.at[:, pl.ds(8, 8)], feat.at[:, bottom], hs.at[0], hr.at[0], {"tile": dn_t}),
        remote(feat.at[:, pl.ds(64, 8)], feat.at[:, top], hs.at[1], hr.at[1], {"tile": up_t}),
        remote(pk, he.at[pl.ds(8, 64)], hs.at[2], hr.at[2], {"depth": dn_d}),
        remote(pk, hw.at[pl.ds(8, 64)], hs.at[3], hr.at[3], {"depth": up_d}),
        remote(pk.at[pl.ds(0, 8)], he.at[bottom], hs.at[4], hr.at[4], {"depth": dn_d, "tile": dn_t}),
        remote(pk.at[pl.ds(56, 8)], he.at[top], hs.at[5], hr.at[5], {"depth": dn_d, "tile": up_t}),
        remote(pk.at[pl.ds(0, 8)], hw.at[bottom], hs.at[6], hr.at[6], {"depth": up_d, "tile": dn_t}),
        remote(pk.at[pl.ds(56, 8)], hw.at[top], hs.at[7], hr.at[7], {"depth": up_d, "tile": up_t}),
    ]
    for copy in halo:
        copy.start()

    def shift_rows(i, carry):
        rows = rows_at(8 * i)
        for p in range(8):
            x = feat[p, rows, :]
            for k in range(SPAN):
                dx = k - RADIUS
                y = pltpu.roll(x, (-dx) % 128, 1) if dx else x
                if p == 4:
                    y = y - dx * dx * (LOG2E / 72.0)
                    if dx:
                        y = jnp.where(lane >= 128 - dx if dx > 0 else lane < -dx, -1e30, y)
                shf[k, p, rows, :] = y
        return carry

    def fall(dy, like):
        rise = (dy - RADIUS).astype(f32)
        return jnp.exp2(like * 0.0 + rise * rise * (-LOG2E / 72.0))

    def add_tap(part, q, twice):
        e = q[4]
        for p in range(4):
            e = e + twice[p] * q[p]
        w = jnp.exp2(e)
        terms = [w * q[5], w * q[6], w * q[7], w]
        return terms if part is None else [u + v for u, v in zip(part, terms)]

    def inside(g, carry):
        twice = [feat[p, rows_at(8 * g + 8), :] * 2.0 for p in range(4)]

        def line(dy, sums):
            rows = pl.ds(8 * g + dy, 8)
            part = None
            for k in range(SPAN):
                part = add_tap(part, [shf[k, p, rows, :] for p in range(8)], twice)
            f = fall(dy, twice[0])
            return tuple(u + f * v for u, v in zip(sums, part))

        sums = lax.fori_loop(0, SPAN, line, (twice[0] * 0.0,) * 4, unroll=4)
        for c in range(4):
            tot[c, rows_at(8 * g), :] = sums[c]
        return carry

    lax.fori_loop(1, 9, shift_rows, 0, unroll=2)
    lax.fori_loop(1, 7, inside, 0)
    for copy in halo:
        copy.wait()

    def absent(i):
        return ((i == 0) & (t == 0)) | ((i == 9) & (t == nt - 1))

    def outer_rows(n, carry):
        i = 9 * n
        rows = rows_at(8 * i)
        feat[4, rows, :] = jnp.where(absent(i), -1e30, feat[4, rows, :])
        shift_rows(i, 0)
        return inside(7 * n, carry)

    lax.fori_loop(0, 2, outer_rows, 0)

    e, m = lane >> 3, lane & 7
    left = e < 8
    column = e + m
    there = jnp.where(left, jnp.where(column <= 7, 1, 0), jnp.where(column >= 15, 1, 0))
    there = there * jnp.where(left, jnp.where(d > 0, 1, 0), jnp.where(d < nd - 1, 1, 0))
    source = jnp.where(left, column & 7, 8 + ((column + 1) & 7))
    run = jnp.where(left, 8 - m, m + 1).astype(f32)
    drop = jnp.where(there == 1, run * run * (-LOG2E / 72.0), -1e30)
    pixel = jnp.where(left, e, 112 + e)
    home = jnp.where(lane < 8, 8 * lane, jnp.where(lane >= 120, 8 * (lane - 112), 0))
    edge_lane = (lane < 8) | (lane >= 120)

    def rim_rows(i, carry):
        rows = rows_at(8 * i)
        both = jnp.where((lane & 15) < 8, hw[rows, :], he[rows, :])
        for p in range(8):
            v = jnp.take_along_axis(both, source + 16 * p, axis=1)
            if p == 4:
                v = jnp.where(absent(i), -1e30, v + drop)
            rim[p, rows, :] = v
        return carry

    lax.fori_loop(0, 10, rim_rows, 0, unroll=5)

    def outside(G, carry):
        groups = [4 * G + i for i in range(4)]
        own = [[feat[p, rows_at(8 * g + 8), :] for p in range(4)] for g in groups]
        twice = [[jnp.take_along_axis(v * 2.0, pixel, axis=1) for v in o] for o in own]
        scale = []
        for o in own:
            norm = o[0] * o[0]
            for v in o[1:]:
                norm = norm + v * v
            scale.append(jnp.exp2(-norm))

        def line(dy, sums):
            f = fall(dy, twice[0][0])
            new = []
            for g, tw, sm in zip(groups, twice, sums):
                part = add_tap(None, [rim[p, pl.ds(8 * g + dy, 8), :] for p in range(8)], tw)
                new.append(tuple(u + f * v for u, v in zip(sm, part)))
            return tuple(new)

        sums = lax.fori_loop(0, SPAN, line, ((twice[0][0] * 0.0,) * 4,) * 4, unroll=17)
        flat = [v for sm in sums for v in sm]
        for step in (1, 2, 4):
            turned = [pltpu.roll(v, 128 - step, 1) for v in flat]
            flat = [v + u for v, u in zip(flat, turned)]
        flat = [jnp.take_along_axis(v, home, axis=1) for v in flat]
        for i, g in enumerate(groups):
            total = [tot[c, rows_at(8 * g), :] + jnp.where(edge_lane, flat[4 * i + c], 0.0) for c in range(4)]
            inv = scale[i] / (1.0 + scale[i] * total[3])
            for c in range(3):
                out_ref[c, rows_at(8 * g), :] = total[c] * inv
        return carry

    lax.fori_loop(0, 2, outside, 0)
    for s in range(4):
        to_sibling(s).wait_send()
    for s in range(3):
        to_chip(s, (2, 1, 3)[s]).wait_send()


def per_device(density, view_flip, tf_coeff):
    i32 = jnp.int32
    dma = pltpu.SemaphoreType.DMA
    image = (8, 64, 128)
    return pl.pallas_call(
        kernel,
        out_shape=jax.ShapeDtypeStruct((3, 64, 128), f32),
        in_specs=[
            pl.BlockSpec(memory_space=pltpu.SMEM),
            pl.BlockSpec(memory_space=pltpu.SMEM),
            pl.BlockSpec(memory_space=pl.ANY),
        ],
        out_specs=pl.BlockSpec(memory_space=pltpu.VMEM),
        scratch_shapes=[
            pltpu.VMEM((8, 32, 64, 128), i32),
            pltpu.VMEM((34, 10, 80, 128), f32),
            pltpu.VMEM((2, 64, 1024), i32),
            pltpu.VMEM((2, 32, 1, 1024), i32),
            pltpu.VMEM((2, 9, 64, 128), f32),
            pltpu.VMEM((8,) + image, f32),
            pltpu.VMEM((4,) + image, f32),
            pltpu.VMEM((4,) + image, f32),
            pltpu.VMEM((8, 80, 128), f32),
            pltpu.VMEM((64, 128), f32),
            pltpu.VMEM((80, 128), f32),
            pltpu.VMEM((80, 128), f32),
            pltpu.VMEM((8, 80, 128), f32),
            pltpu.VMEM((SPAN, 8, 80, 128), f32),
            pltpu.VMEM((4, 64, 128), f32),
            dma((8,)),
            dma((2,)), dma((2,)),
            dma((2,)), dma((2,)),
            dma((4,)), dma((4,)),
            dma((4,)), dma((4,)),
            dma((8,)), dma((8,)),
        ],
        compiler_params=pltpu.CompilerParams(
            collective_id=0, has_side_effects=True, vmem_limit_bytes=60 * 1024 * 1024
        ),
        name="render",
    )(view_flip, tf_coeff, density)


def solution(mesh):
    in_specs = (P("depth", "tile", None), P("tile"), P())
    out_specs = P(None, "tile", "depth")
    return jax.shard_map(per_device, mesh=mesh, in_specs=in_specs, out_specs=out_specs, check_vma=False)
```

```python
import jax
import jax.numpy as jnp
from jax import lax
from jax.experimental import pallas as pl
from jax.experimental.pallas import tpu as pltpu
from jax.sharding import PartitionSpec as P

f32 = jnp.float32
LOG2E = 1.4426950408889634
LIGHT = (0.48, 0.6, 0.64)
RADIUS = 8
SPAN = 2 * RADIUS + 1
BANDS = 2


def rows_at(start, count=8):
    return pl.ds(pl.multiple_of(start, 8), count)


def poly(a, x):
    return a[0] + x * (a[1] + x * (a[2] + x * a[3]))


def level_coeffs(tf):
    s = 2.0 / 255.0
    table = []
    for q in range(4):
        c0, c1, c2, c3 = (tf[q, i] for i in range(4))
        m = LOG2E if q == 0 else 0.5
        table.append(
            (
                (c0 - c1 + c2 - c3) * m,
                (c1 - 2.0 * c2 + 3.0 * c3) * (s * m),
                (c2 - 3.0 * c3) * (s * s * m),
                c3 * (s * s * s * m),
            )
        )
    return table


def kernel(flip_ref, tf_ref, dens, out_ref, raw, fld, zh, rh, inner, image, sibr, parts, feat, pk, hw, he, rim, shf, tot,
           load_sem, zs, zr, rs, rr, ss, sr, cs, cr, hs, hr):
    nd, nt = 8, 32
    d, t = lax.axis_index("depth"), lax.axis_index("tile")
    core, chip = d % 2, d // 2
    flip = flip_ref[0]
    flipped = flip == 1
    cells = dens.shape[0]
    up_d, dn_d = (d + 1) % nd, (d + nd - 1) % nd
    up_t, dn_t = (t + 1) % nt, (t + nt - 1) % nt
    sib = 2 * chip + 1 - core

    def load(i):
        j = (2 * ((chip + 2) % 4) + 7 + i) % 8
        piece = dens.at[:, :, pl.ds(pl.multiple_of(128 * j, 128), 128)]
        return j, pltpu.make_async_copy(piece, raw.at[j], load_sem.at[i])

    for i in range(8):
        load(i)[1].start()

    barrier = pltpu.get_barrier_semaphore()
    near = [{"depth": up_d}, {"depth": dn_d}, {"tile": up_t}, {"tile": dn_t}]
    near += [{"depth": a, "tile": b} for a in (up_d, dn_d) for b in (up_t, dn_t)]
    near += [{"depth": (d + 2 * e) % nd} for e in (1, 2, 3)]
    for who in near:
        pl.semaphore_signal(barrier, inc=1, device_id=who, device_id_type=pl.DeviceIdType.MESH)

    def clear(z, carry):
        for j in (0, 9):
            for g in range(8):
                fld[z + 1, j, 8 * g + 8 : 8 * g + 16, :] = jnp.zeros((8, 128), f32)
        return carry

    lax.fori_loop(0, cells, clear, 0)
    pl.semaphore_wait(barrier, len(near))

    def remote(src, dst, send, recv, who):
        return pltpu.make_async_remote_copy(src_ref=src, dst_ref=dst, send_sem=send, recv_sem=recv, device_id=who,
                                            device_id_type=pl.DeviceIdType.MESH)

    edge = [
        remote(dens.at[cells - 1], zh.at[0], zs.at[0], zr.at[0], {"depth": up_d}),
        remote(dens.at[0], zh.at[1], zs.at[1], zr.at[1], {"depth": dn_d}),
        remote(dens.at[:, pl.ds(63, 1)], rh.at[0], rs.at[0], rr.at[0], {"tile": up_t}),
        remote(dens.at[:, pl.ds(0, 1)], rh.at[1], rs.at[1], rr.at[1], {"tile": dn_t}),
    ]
    for copy in edge:
        copy.start()

    lane = lax.broadcasted_iota(jnp.int32, (8, 128), 1)
    first_lane, last_lane = lane == 0, lane == 127
    a = level_coeffs(tf_ref)
    sgn = jnp.where(flipped, -1, 1)
    sf = jnp.where(flipped, -1.0, 1.0)
    z0 = jnp.where(flipped, cells + 1, 0)
    lx, ly, lz = (0.65 / 0.35 * c for c in LIGHT)
    lz = lz * sf
    order = jnp.where(flipped, nd - 1 - d, d).astype(f32)
    h0 = order * (cells / 256.0) + 0.5 / 256.0
    h1 = h0 + (cells - 1) / 256.0

    def place(b, i):
        return 8 * ((BANDS * b + 1 + i) % 8)

    def cell(j, b):
        def body(k, state):
            zc = z0 + sgn * (k + 1)
            new = []
            for i in range(BANDS):
                prev, cur, S, T, sums, aw, c1, c2, c3, nx, ny, nl = state[i]
                r0 = place(b, i)
                rows = rows_at(r0 + 8)
                nxt = fld[zc + sgn, j, rows, :]
                right, left = fld[zc, j + 1, rows, :], fld[zc, j - 1, rows, :]
                ahead = pltpu.roll(jnp.where(first_lane, right, cur), 127, 1)
                behind = pltpu.roll(jnp.where(last_lane, left, cur), 1, 1)
                gx = ahead - behind
                gy = fld[zc, j, pl.ds(r0 + 9, 8), :] - fld[zc, j, pl.ds(r0 + 7, 8), :]
                gz = nxt - prev
                r = lax.rsqrt((gx * gx + gy * gy) + (gz * gz + 65025.0))
                S = S + jnp.log2(1.0 + jnp.exp2(poly(a[0], cur)))
                after = jnp.exp2(S * -0.008)
                w = T - after
                sums = sums + T
                wr = w * r
                lit = wr * (gx * lx + gy * ly + gz * lz)
                ws = w + jnp.abs(lit)
                aw = aw + ws
                c1 = c1 + ws * jnp.tanh(poly(a[1], cur))
                c2 = c2 + ws * jnp.tanh(poly(a[2], cur))
                c3 = c3 + ws * jnp.tanh(poly(a[3], cur))
                nx = nx + wr * gx
                ny = ny + wr * gy
                nl = nl + lit
                new.append((cur, nxt, S, after, sums, aw, c1, c2, c3, nx, ny, nl))
            return tuple(new)

        return body

    def enter(j, b, k):
        start = []
        for i in range(BANDS):
            rows = rows_at(place(b, i) + 8)
            prev, cur = fld[z0 + sgn * k, j, rows, :], fld[z0 + sgn * (k + 1), j, rows, :]
            zero = cur * 0.0
            start.append((prev, cur, zero, zero + 1.0) + (zero,) * 8)
        return tuple(start)

    def leave(state, b, slot):
        for i in range(BANDS):
            _, _, _, T, sums, aw, c1, c2, c3, nx, ny, nl = state[i]
            nz = (nl - lx * nx - ly * ny) * (0.35 / 0.65 / LIGHT[2])
            height = (h0 - 1.0 / 256.0) + sums * (1.0 / 256.0) - T * h1
            planes = (0.175 * (aw + c1), 0.175 * (aw + c2), 0.175 * (aw + c3), T, height, nx, ny, nz)
            for p in range(8):
                image[slot, p, rows_at(place(b, i)), :] = planes[p]

    def offset(s):
        return (10 - s + 3 * (s * (s - 1) // 2)) % 4

    def block_of(h):
        return 2 * ((chip + offset(h // 2)) % 4) + (h + core + 1) % 2 + 1

    def take(i, carry):
        j, copy = load(i)
        copy.wait()

        def layer(z, c):
            for g in range(8):
                fld[z + 1, j + 1, 8 * g + 8 : 8 * g + 16, :] = raw[j, z, 8 * g : 8 * g + 8, :].astype(f32)
            return c

        return lax.fori_loop(0, cells, layer, carry, unroll=8)

    lax.fori_loop(0, 4, take, 0)

    def early(n, carry):
        h, b = n // 3, n % 3
        j = block_of(h)
        done = lax.fori_loop(1, cells - 1, cell(j, b), enter(j, b, 1), unroll=30)
        for i in range(BANDS):
            for q, v in enumerate(done[i][2:3] + done[i][4:]):
                inner[h, q, rows_at(place(b, i)), :] = v
        return carry

    lax.fori_loop(0, 6, early, 0)
    lax.fori_loop(4, 8, take, 0)
    for copy in edge:
        copy.wait()

    keep = [jnp.where(d > 0, 1.0, 0.0), jnp.where(d < nd - 1, 1.0, 0.0)]
    keep_row = [jnp.where(t > 0, 1.0, 0.0), jnp.where(t < nt - 1, 1.0, 0.0)]

    def fill_planes(g, carry):
        for side, layer in ((0, 0), (1, cells + 1)):
            for j in range(8):
                v = zh[side, rows_at(8 * g), 128 * j : 128 * j + 128].astype(f32)
                fld[layer, j + 1, rows_at(8 * g + 8), :] = v * keep[side]
        return carry

    lax.fori_loop(0, 8, fill_planes, 0)

    def fill_rows(z, carry):
        for side, row in ((0, 7), (1, 72)):
            for j in range(8):
                v = rh[side, z, :, 128 * j : 128 * j + 128].astype(f32)
                fld[z + 1, j + 1, row : row + 1, :] = v * keep_row[side]
        return carry

    lax.fori_loop(0, cells, fill_rows, 0, unroll=2)

    own_front = core == flip

    def to_sibling(s):
        return remote(image.at[2 * s], sibr.at[s], ss.at[s], sr.at[s], {"depth": sib})

    def to_chip(s, e):
        return remote(image.at[2 * s + 1], parts.at[(4 - e) % 4], cs.at[s], cr.at[(4 - e) % 4],
                      {"depth": (d + 2 * e) % nd})

    def half_step(h, carry):
        j = block_of(h)
        s = h // 2

        def bands(b, c):
            resumed = (h < 2) & (b < 3)

            @pl.when(resumed)
            def _():
                body = cell(j, b)
                state = body(0, enter(j, b, 0))
                mixed = []
                for i in range(BANDS):
                    _, _, S, T, *sums = state[i]
                    rows = rows_at(place(b, i))
                    mid = [inner[h, q, rows, :] for q in range(9)]
                    S = S + mid[0]
                    sums = [v + T * m for v, m in zip(sums, mid[1:])]
                    tail = rows_at(place(b, i) + 8)
                    prev, cur = fld[z0 + sgn * (cells - 1), j, tail, :], fld[z0 + sgn * cells, j, tail, :]
                    mixed.append((prev, cur, S, jnp.exp2(S * -0.008), *sums))
                leave(body(cells - 1, tuple(mixed)), b, h)

            @pl.when(jnp.logical_not(resumed))
            def _():
                leave(lax.fori_loop(0, cells, cell(j, b), enter(j, b, 0), unroll=32), b, h)

            return c

        lax.fori_loop(0, 8 // BANDS, bands, 0)

        @pl.when(h % 2 == 0)
        def _():
            to_sibling(s).start()

        @pl.when(h % 2 == 1)
        def _():
            to_sibling(s).wait_recv()

            def merge(g, c):
                rows = rows_at(8 * g)
                x = [image[h, p, rows, :] for p in range(8)]
                y = [sibr[s, p, rows, :] for p in range(8)]
                front = [jnp.where(own_front, x[p], y[p]) for p in range(8)]
                back = [jnp.where(own_front, y[p], x[p]) for p in range(8)]
                for p in range(8):
                    image[h, p, rows, :] = front[3] * back[p] if p == 3 else front[p] + front[3] * back[p]
                return c

            lax.fori_loop(0, 8, merge, 0, unroll=2)

            @pl.when(s < 3)
            def _():
                to_chip(s, offset(s)).start()

        return carry

    lax.fori_loop(0, 8, half_step, 0)
    for s in range(3):
        to_chip(s, (2, 1, 3)[s]).wait_recv()

    kd, kn = (20.0 * LOG2E) ** 0.5, (2.0 * LOG2E) ** 0.5

    def finish(g, carry):
        rows = rows_at(8 * g)

        def part(i):
            who = jnp.where(flipped, 3 - i, i)
            slot = (who - chip + 4) % 4
            inside = slot == 0
            return [jnp.where(inside, image[7, p, rows, :], parts[slot, p, rows, :]) for p in range(8)]

        acc = part(0)
        for i in range(1, 4):
            back = part(i)
            acc = [acc[3] * back[p] if p == 3 else acc[p] + acc[3] * back[p] for p in range(8)]
        nx, ny, nz = acc[5:8]
        facing = jnp.maximum(LIGHT[0] * nx + LIGHT[1] * ny + LIGHT[2] * nz, 0.0)
        glow = 0.4 + 0.6 * facing
        f = [acc[4] * kd, nx * kn, ny * kn, nz * kn]
        bias = jnp.log2(jnp.maximum(1.0 - acc[3], 1e-37))
        for v in f:
            bias = bias - v * v
        f += [bias] + [acc[p] * glow for p in range(3)]
        packed = pltpu.roll(f[0], 8, 1)
        for p in range(8):
            feat[p, rows_at(8 * g + 8), :] = f[p]
            if p:
                packed = jnp.where(lane >= 16 * p, pltpu.roll(f[p], 16 * p + 8, 1), packed)
        pk[rows, :] = packed
        return carry

    lax.fori_loop(0, 8, finish, 0, unroll=4)

    top, bottom = pl.ds(0, 8), pl.ds(72, 8)
    halo = [
        remote(feat.at[:, pl.ds(8, 8)], feat.at[:, bottom], hs.at[0], hr.at[0], {"tile": dn_t}),
        remote(feat.at[:, pl.ds(64, 8)], feat.at[:, top], hs.at[1], hr.at[1], {"tile": up_t}),
        remote(pk, he.at[pl.ds(8, 64)], hs.at[2], hr.at[2], {"depth": dn_d}),
        remote(pk, hw.at[pl.ds(8, 64)], hs.at[3], hr.at[3], {"depth": up_d}),
        remote(pk.at[pl.ds(0, 8)], he.at[bottom], hs.at[4], hr.at[4], {"depth": dn_d, "tile": dn_t}),
        remote(pk.at[pl.ds(56, 8)], he.at[top], hs.at[5], hr.at[5], {"depth": dn_d, "tile": up_t}),
        remote(pk.at[pl.ds(0, 8)], hw.at[bottom], hs.at[6], hr.at[6], {"depth": up_d, "tile": dn_t}),
        remote(pk.at[pl.ds(56, 8)], hw.at[top], hs.at[7], hr.at[7], {"depth": up_d, "tile": up_t}),
    ]
    for copy in halo:
        copy.start()

    def shift_rows(i, carry):
        rows = rows_at(8 * i)
        for p in range(8):
            x = feat[p, rows, :]
            for k in range(SPAN):
                dx = k - RADIUS
                y = pltpu.roll(x, (-dx) % 128, 1) if dx else x
                if p == 4:
                    y = y - dx * dx * (LOG2E / 72.0)
                    if dx:
                        y = jnp.where(lane >= 128 - dx if dx > 0 else lane < -dx, -1e30, y)
                shf[k, p, rows, :] = y
        return carry

    def fall(dy, like):
        rise = (dy - RADIUS).astype(f32)
        return jnp.exp2(like * 0.0 + rise * rise * (-LOG2E / 72.0))

    def add_tap(part, q, twice):
        e = q[4]
        for p in range(4):
            e = e + twice[p] * q[p]
        w = jnp.exp2(e)
        terms = [w * q[5], w * q[6], w * q[7], w]
        return terms if part is None else [u + v for u, v in zip(part, terms)]

    def inside(g, carry):
        twice = [feat[p, rows_at(8 * g + 8), :] * 2.0 for p in range(4)]

        def line(dy, sums):
            rows = pl.ds(8 * g + dy, 8)
            part = None
            for k in range(SPAN):
                part = add_tap(part, [shf[k, p, rows, :] for p in range(8)], twice)
            f = fall(dy, twice[0])
            return tuple(u + f * v for u, v in zip(sums, part))

        sums = lax.fori_loop(0, SPAN, line, (twice[0] * 0.0,) * 4, unroll=4)
        for c in range(4):
            tot[c, rows_at(8 * g), :] = sums[c]
        return carry

    lax.fori_loop(1, 9, shift_rows, 0, unroll=4)
    lax.fori_loop(1, 7, inside, 0)
    for copy in halo:
        copy.wait()

    def absent(i):
        return ((i == 0) & (t == 0)) | ((i == 9) & (t == nt - 1))

    def outer_rows(n, carry):
        i = 9 * n
        rows = rows_at(8 * i)
        feat[4, rows, :] = jnp.where(absent(i), -1e30, feat[4, rows, :])
        shift_rows(i, 0)
        return inside(7 * n, carry)

    lax.fori_loop(0, 2, outer_rows, 0)

    e, m = lane >> 3, lane & 7
    left = e < 8
    column = e + m
    there = jnp.where(left, jnp.where(column <= 7, 1, 0), jnp.where(column >= 15, 1, 0))
    there = there * jnp.where(left, jnp.where(d > 0, 1, 0), jnp.where(d < nd - 1, 1, 0))
    source = jnp.where(left, column & 7, 8 + ((column + 1) & 7))
    run = jnp.where(left, 8 - m, m + 1).astype(f32)
    drop = jnp.where(there == 1, run * run * (-LOG2E / 72.0), -1e30)
    pixel = jnp.where(left, e, 112 + e)
    home = jnp.where(lane < 8, 8 * lane, jnp.where(lane >= 120, 8 * (lane - 112), 0))
    edge_lane = (lane < 8) | (lane >= 120)

    def rim_rows(i, carry):
        rows = rows_at(8 * i)
        both = jnp.where((lane & 15) < 8, hw[rows, :], he[rows, :])
        for p in range(8):
            v = jnp.take_along_axis(both, source + 16 * p, axis=1)
            if p == 4:
                v = jnp.where(absent(i), -1e30, v + drop)
            rim[p, rows, :] = v
        return carry

    lax.fori_loop(0, 10, rim_rows, 0, unroll=10)

    def outside(G, carry):
        groups = [4 * G + i for i in range(4)]
        own = [[feat[p, rows_at(8 * g + 8), :] for p in range(4)] for g in groups]
        twice = [[jnp.take_along_axis(v * 2.0, pixel, axis=1) for v in o] for o in own]
        scale = []
        for o in own:
            norm = o[0] * o[0]
            for v in o[1:]:
                norm = norm + v * v
            scale.append(jnp.exp2(-norm))

        def line(dy, sums):
            f = fall(dy, twice[0][0])
            new = []
            for g, tw, sm in zip(groups, twice, sums):
                part = add_tap(None, [rim[p, pl.ds(8 * g + dy, 8), :] for p in range(8)], tw)
                new.append(tuple(u + f * v for u, v in zip(sm, part)))
            return tuple(new)

        sums = lax.fori_loop(0, SPAN, line, ((twice[0][0] * 0.0,) * 4,) * 4, unroll=17)
        flat = [v for sm in sums for v in sm]
        for step in (1, 2, 4):
            turned = [pltpu.roll(v, 128 - step, 1) for v in flat]
            flat = [v + u for v, u in zip(flat, turned)]
        flat = [jnp.take_along_axis(v, home, axis=1) for v in flat]
        for i, g in enumerate(groups):
            total = [tot[c, rows_at(8 * g), :] + jnp.where(edge_lane, flat[4 * i + c], 0.0) for c in range(4)]
            inv = scale[i] / (1.0 + scale[i] * total[3])
            for c in range(3):
                out_ref[c, rows_at(8 * g), :] = total[c] * inv
        return carry

    lax.fori_loop(0, 2, outside, 0, unroll=2)
    for s in range(4):
        to_sibling(s).wait_send()
    for s in range(3):
        to_chip(s, (2, 1, 3)[s]).wait_send()


def per_device(density, view_flip, tf_coeff):
    i32 = jnp.int32
    dma = pltpu.SemaphoreType.DMA
    image = (8, 64, 128)
    return pl.pallas_call(
        kernel,
        out_shape=jax.ShapeDtypeStruct((3, 64, 128), f32),
        in_specs=[
            pl.BlockSpec(memory_space=pltpu.SMEM),
            pl.BlockSpec(memory_space=pltpu.SMEM),
            pl.BlockSpec(memory_space=pl.ANY),
        ],
        out_specs=pl.BlockSpec(memory_space=pltpu.VMEM),
        scratch_shapes=[
            pltpu.VMEM((8, 32, 64, 128), i32),
            pltpu.VMEM((34, 10, 80, 128), f32),
            pltpu.VMEM((2, 64, 1024), i32),
            pltpu.VMEM((2, 32, 1, 1024), i32),
            pltpu.VMEM((2, 9, 64, 128), f32),
            pltpu.VMEM((8,) + image, f32),
            pltpu.VMEM((4,) + image, f32),
            pltpu.VMEM((4,) + image, f32),
            pltpu.VMEM((8, 80, 128), f32),
            pltpu.VMEM((64, 128), f32),
            pltpu.VMEM((80, 128), f32),
            pltpu.VMEM((80, 128), f32),
            pltpu.VMEM((8, 80, 128), f32),
            pltpu.VMEM((SPAN, 8, 80, 128), f32),
            pltpu.VMEM((4, 64, 128), f32),
            dma((8,)),
            dma((2,)), dma((2,)),
            dma((2,)), dma((2,)),
            dma((4,)), dma((4,)),
            dma((4,)), dma((4,)),
            dma((8,)), dma((8,)),
        ],
        compiler_params=pltpu.CompilerParams(
            collective_id=0, has_side_effects=True, vmem_limit_bytes=60 * 1024 * 1024
        ),
        name="render",
    )(view_flip, tf_coeff, density)


def solution(mesh):
    in_specs = (P("depth", "tile", None), P("tile"), P())
    out_specs = P(None, "tile", "depth")
    return jax.shard_map(per_device, mesh=mesh, in_specs=in_specs, out_specs=out_specs, check_vma=False)
```
